256 devices in a mesh: row: 8 (over x, y_lo), col: 32 (over y_hi, z, core).
Axes of the slice: x: 4, y: 4 (y_hi: 2, y_lo: 2; y = y_hi * 2 + y_lo), z: 8, core: 2. Of those that a mesh axis runs over, the one named last changes fastest.
Arguments:
- features: bfloat16 [32768, 512], P(('col', 'row')), may hold values from -6 to 6
- tile_vals: bfloat16 [8, 4096, 128, 128], P('row', 'col')
- tile_row: int32 [8, 4096], P('row', 'col'), may hold values from 0 to 31
- tile_col: int32 [8, 4096], P('row', 'col'), may hold values from 0 to 7
- tile_count: int32 [8, 32], P('row', 'col'), may hold values from 1 to 128, as said below
- node_type: int32 [32768], P(('row', 'col')), may hold values from 0 to 7
- type_gain: float32 [8, 512], replicated, may hold values from 0.1 to 1.9
- w_in: bfloat16 [512, 1024], replicated, may hold values from -0.25 to 0.25
- w_out: bfloat16 [1024, 512], replicated, may hold values from -0.1875 to 0.1875
- cotangent: bfloat16 [32768, 512], P(('row', 'col')), may hold values from -6 to 6
Outputs:
- mixed: bfloat16 [32768, 512], P(('row', 'col'))
- grad_x: float32 [32768, 512], P(('col', 'row'))
- grad_w_in: float32 [512, 1024], replicated
- grad_w_out: float32 [1024, 512], replicated
- grad_gain: float32 [8, 512], replicated
The draws below stay inside these ranges and needn't reach their ends.
Inputs may be any that keep to these rules, and one draw needn't show every extreme that they name: Slots 0 to tile_count - 1 of a grid cell's list are live; some grid cell has all 128 slots live in every draw.
All inputs are finite; a program needn't handle non-finite values.
Results may differ from the reference program's by a relative error of at most 0.0056.
Values may be sent and summed in bfloat16 or wider, within the bound.
A program may use at most 128 MiB of HBM per device.

```python
import jax
import jax.numpy as jnp
from jax import lax

F = 512
HID = 1024
TYPES = 8
TILE = 128
TILES = 128
NODES = 32768
N_ROW = 8
N_COL = 32


def draw_tile_vals(key, part):
    base_key, keep_key = jax.random.split(jax.random.fold_in(key, 7), 2)
    shape = (N_ROW, N_COL * TILES, TILE, TILE)
    spread = (4.0 / (0.75 * TILE * TILES)) ** 0.5
    keeping = (jax.random.randint(keep_key, shape, 0, 4) > 0).astype(jnp.float32)
    values_drawn = jax.random.normal(base_key, shape, jnp.float32)
    return (values_drawn * keeping * spread).astype(jnp.bfloat16)


def draw_tile_count(key, part):
    first_key, second_key, pick_key = jax.random.split(jax.random.fold_in(key, 11), 3)
    first = jax.random.randint(first_key, (N_ROW * N_COL,), 1, TILES + 1)
    second = jax.random.randint(second_key, (N_ROW * N_COL,), 1, TILES + 1)
    counts = jnp.maximum(first * second // TILES, 1)
    chosen = jax.random.randint(pick_key, (), 0, N_ROW * N_COL)
    counts = jnp.where(jnp.arange(N_ROW * N_COL, dtype=jnp.int32) == chosen, TILES, counts)
    return counts.reshape(N_ROW, N_COL).astype(jnp.int32)


def set_ends(drawn, own_key, least, top_value):
    shape = drawn.shape
    place = [jax.random.randint(jax.random.fold_in(own_key, axis), (), 0, shape[axis]) for axis in range(len(shape))]
    drawn = drawn.at[tuple(place)].set(least)
    longest = shape.index(max(shape))
    place[longest] = (place[longest] + 1) % shape[longest]
    return drawn.at[tuple(place)].set(top_value)


def levels(key, extent, shards, smallest, top_value):
    def one(position, parts):
        steps = jax.random.uniform(jax.random.fold_in(jax.random.fold_in(key, 6), position), (parts,), jnp.float32, smallest / len(shards), top_value / len(shards))
        return jnp.repeat(jnp.exp(steps), extent[position] // parts).reshape((-1,) + (1,) * (len(extent) - position - 1))

    gain = one(*shards[0])
    for cut in shards[1:]:
        gain = gain * one(*cut)
    return gain


def noise(key, shape, width, reach, cuts=(), held_as=jnp.bfloat16):
    array = width * jax.random.normal(key, shape, jnp.float32)
    if cuts:
        array = array * levels(key, shape, cuts, -0.22, 0.18)
    return jnp.clip(array, -reach, reach).astype(held_as)


def setup_inputs(seed: int = 0) -> dict:
    seeds = jax.random.split(jax.random.key(seed), 11)
    features = noise(seeds[0], (NODES, F), 1.0, 6.0, ((0, 256),))
    tile_vals = draw_tile_vals(jax.random.fold_in(seeds[10], 71), 0)
    tile_row = set_ends(jax.random.randint(seeds[2], (N_ROW, N_COL * TILES), 0, N_COL), jax.random.fold_in(seeds[2], 1), 0, N_COL - 1).astype(jnp.int32)
    tile_col = set_ends(jax.random.randint(seeds[3], (N_ROW, N_COL * TILES), 0, N_ROW), jax.random.fold_in(seeds[3], 1), 0, N_ROW - 1).astype(jnp.int32)
    tile_count = draw_tile_count(jax.random.fold_in(seeds[10], 71), 0)
    node_type = set_ends(jax.random.randint(seeds[5], (NODES,), 0, TYPES), jax.random.fold_in(seeds[5], 1), 0, TYPES - 1).astype(jnp.int32)
    type_gain = jnp.clip(1.0 + 0.18 * jax.random.normal(seeds[6], (TYPES, F), jnp.float32), 0.1, 1.9)
    w_in = noise(seeds[7], (F, HID), F ** -0.5, 0.25)
    w_out = noise(seeds[8], (HID, F), HID ** -0.5, 0.1875)
    cotangent = noise(seeds[9], (NODES, F), 1.0, 6.0, ((0, 256),))
    return dict(features=features, tile_vals=tile_vals, tile_row=tile_row, tile_col=tile_col, tile_count=tile_count, node_type=node_type, type_gain=type_gain, w_in=w_in, w_out=w_out, cotangent=cotangent)


def reference(features, tile_vals, tile_row, tile_col, tile_count, node_type, type_gain, w_in, w_out, cotangent):
    total_nodes = TILE * N_ROW * N_COL
    blocks = N_COL * TILES // 16
    panels = features.reshape(N_COL, N_ROW, TILE, F).astype(jnp.float32)
    slot_ids = jnp.arange(N_COL * TILES, dtype=jnp.int32)
    owner_col = (slot_ids // TILES).astype(jnp.int32)
    owner_blocks = owner_col.reshape(blocks, 16)

    def living_slots(counts_row):
        return (slot_ids % TILES < counts_row[owner_col]).reshape(blocks, 16)

    def gather_rows(inputs):
        weights_row, rows_row, cols_row, counts_row = inputs
        living = living_slots(counts_row)

        def advance(totals, pieces):
            weights_now, row_ids, col_ids, owners, alive = pieces
            sources = panels[owners, col_ids]
            product = jnp.einsum('sab,sbf->saf', weights_now.astype(jnp.float32), sources, precision=lax.Precision.HIGHEST)
            product = jnp.where(alive[:, None, None], product, 0.0)
            return (totals.at[row_ids].add(product), None)
        start = jnp.zeros((N_COL, TILE, F), jnp.float32)
        totals, unused = lax.scan(advance, start, (weights_row.reshape(blocks, 16, TILE, TILE), rows_row.reshape(blocks, 16), cols_row.reshape(blocks, 16), owner_blocks, living))
        return totals
    aggregate = lax.map(gather_rows, (tile_vals, tile_row, tile_col, tile_count)).reshape(total_nodes, F)
    center = lax.optimization_barrier(jnp.mean(aggregate, axis=-1, keepdims=True))
    spread = lax.optimization_barrier(jnp.mean(jnp.square(aggregate - center), axis=-1, keepdims=True))
    inverse = lax.rsqrt(spread + 1e-05)
    normed = (aggregate - center) * inverse
    onehot = (node_type[:, None] == jnp.arange(TYPES, dtype=jnp.int32)[None, :]).astype(jnp.float32)
    gains = jnp.dot(onehot, type_gain, precision=lax.Precision.HIGHEST)
    scaled = (normed * gains).astype(jnp.bfloat16)
    hidden = jnp.dot(scaled, w_in, preferred_element_type=jnp.float32)
    activated = jax.nn.silu(hidden).astype(jnp.bfloat16)
    branch = jnp.dot(activated, w_out, preferred_element_type=jnp.float32)
    mixed = (aggregate + branch).astype(jnp.bfloat16)
    upstream = cotangent.astype(jnp.float32)
    grad_out_w = jnp.dot(activated.T, cotangent, preferred_element_type=jnp.float32)
    grad_act = jnp.dot(cotangent, w_out.T, preferred_element_type=jnp.float32)
    sigmoid_h = jax.nn.sigmoid(hidden)
    grad_hidden = (grad_act * sigmoid_h * (1.0 + hidden * (1.0 - sigmoid_h))).astype(jnp.bfloat16)
    grad_in_w = jnp.dot(scaled.T, grad_hidden, preferred_element_type=jnp.float32)
    grad_scaled = jnp.dot(grad_hidden, w_in.T, preferred_element_type=jnp.float32)
    grad_gain = jnp.dot(onehot.T, grad_scaled * normed, precision=lax.Precision.HIGHEST)
    grad_normed = grad_scaled * gains
    grad_agg = upstream + inverse * (grad_normed - lax.optimization_barrier(jnp.mean(grad_normed, axis=-1, keepdims=True)) - normed * lax.optimization_barrier(jnp.mean(grad_normed * normed, axis=-1, keepdims=True)))
    grad_rows = grad_agg.astype(jnp.bfloat16)
    grad_blocks = grad_rows.reshape(N_ROW, N_COL, TILE, F).astype(jnp.float32)

    def scatter_rows(totals, inputs):
        weights_row, rows_row, cols_row, counts_row, grads_row = inputs
        living = living_slots(counts_row)

        def advance(inner, pieces):
            weights_now, row_ids, col_ids, owners, alive = pieces
            sources = grads_row[row_ids]
            product = jnp.einsum('sab,saf->sbf', weights_now.astype(jnp.float32), sources, precision=lax.Precision.HIGHEST)
            product = jnp.where(alive[:, None, None], product, 0.0)
            return (inner.at[owners, col_ids].add(product), None)
        totals, unused = lax.scan(advance, totals, (weights_row.reshape(blocks, 16, TILE, TILE), rows_row.reshape(blocks, 16), cols_row.reshape(blocks, 16), owner_blocks, living))
        return (totals, None)
    start = jnp.zeros((N_COL, N_ROW, TILE, F), jnp.float32)
    grad_panels, unused = lax.scan(scatter_rows, start, (tile_vals, tile_row, tile_col, tile_count, grad_blocks))
    grad_x = grad_panels.reshape(total_nodes, F)
    factor = float(total_nodes) ** (-0.5)
    return (mixed, grad_x, grad_in_w * factor, grad_out_w * factor, grad_gain * factor)
```

```python
import functools

import jax
import jax.numpy as jnp
from jax import lax
from jax.experimental import pallas as pl
from jax.experimental.pallas import tpu as pltpu
from jax.sharding import PartitionSpec as P

F = 512
TYPES = 8
TILE = 128
GROUP = 16
UNROLL = 4
HALF = TILE // 2
MESH = pl.DeviceIdType.MESH
BF = jnp.bfloat16
F32 = jnp.float32


def sweep_body(forward, spare, count, rows, cols, weights, sources, out, acc):
    step = pl.program_id(0)

    @pl.when(step == 0)
    def _():
        acc[...] = jnp.zeros_like(acc)

    first = step * GROUP
    live = count[0]
    rounds = jnp.clip((live - first + UNROLL - 1) // UNROLL, 0, GROUP // UNROLL)

    def advance(block, carry):
        products = []
        places = []
        for u in range(UNROLL):
            inner = block * UNROLL + u
            slot = first + inner
            source, place = (cols[slot], rows[slot]) if forward else (rows[slot], cols[slot])
            places.append(jnp.where(slot < live, place, spare))
            contract = ((1,), (0,)) if forward else ((0,), (0,))
            products.append(
                lax.dot_general(
                    weights[inner],
                    sources[source],
                    (contract, ((), ())),
                    preferred_element_type=jnp.float32,
                )
            )
        for place, product in zip(places, products):
            acc[place] += product
        return carry

    lax.fori_loop(0, rounds, advance, 0)

    @pl.when(step == pl.num_programs(0) - 1)
    def _():
        for tile in range(spare):
            out[tile] = acc[tile].astype(out.dtype)


def sweep(weights_all, row_ids, col_ids, live_count, sources, spare, forward, dtype):
    slots = weights_all.shape[0]
    last = lambda count: (count[0] - 1) // GROUP
    return pl.pallas_call(
        functools.partial(sweep_body, forward, spare),
        grid_spec=pltpu.PrefetchScalarGridSpec(
            num_scalar_prefetch=3,
            grid=(slots // GROUP,),
            in_specs=[
                pl.BlockSpec(
                    (GROUP, TILE, TILE), lambda i, n, r, c: (jnp.minimum(i, last(n)), 0, 0)
                ),
                pl.BlockSpec(sources.shape, lambda i, n, r, c: (0, 0, 0)),
            ],
            out_specs=pl.BlockSpec((spare, TILE, F), lambda i, n, r, c: (0, 0, 0)),
            scratch_shapes=[pltpu.VMEM((spare + 1, TILE, F), jnp.float32)],
        ),
        out_shape=jax.ShapeDtypeStruct((spare, TILE, F), dtype),
        name="sweep_forward" if forward else "sweep_backward",
    )(live_count, row_ids, col_ids, weights_all, sources)


class Place:
    def __init__(self):
        row = lax.axis_index("row")
        col = lax.axis_index("col")
        self.row, self.col = row, col
        self.x, self.low = row // 2, row % 2
        self.high, self.z, self.core = col // 16, (col // 2) % 8, col % 2
        self.y = self.high * 2 + self.low

    def at(self, x=None, y=None, z=None, core=None):
        x = self.x if x is None else x
        y = self.y if y is None else y
        z = self.z if z is None else z
        core = self.core if core is None else core
        return (x * 2 + y % 2, (y // 2) * 16 + z * 2 + core)

    def along(self, axis, offset):
        size = {"x": 4, "y": 4, "z": 8}[axis]
        return self.at(**{axis: (getattr(self, axis) + offset + size) % size})


class Wire:
    def __init__(self, send, recv):
        self.send, self.recv, self.copies = send, recv, []

    def push(self, source, target, device):
        index = len(self.copies)
        copy = pltpu.make_async_remote_copy(
            src_ref=source,
            dst_ref=target,
            send_sem=self.send.at[index],
            recv_sem=self.recv.at[index],
            device_id=device,
            device_id_type=MESH,
        )
        copy.start()
        self.copies.append([copy, False])
        return index

    def arrived(self, index):
        if not self.copies[index][1]:
            self.copies[index][0].wait_recv()
            self.copies[index][1] = True

    def finish(self):
        for index, (copy, _) in enumerate(self.copies):
            self.arrived(index)
            copy.wait_send()


def enter(devices):
    barrier = pltpu.get_barrier_semaphore()
    for device in devices:
        pl.semaphore_signal(barrier, inc=1, device_id=device, device_id_type=MESH)
    pl.semaphore_wait(barrier, len(devices))


def halves(size):
    return (pl.ds(0, size // 2), pl.ds(size // 2, size // 2))


def remote_call(body, name, ident, outs, in_spaces, scratch, copies, args):
    return pl.pallas_call(
        body,
        out_shape=outs,
        in_specs=[pl.BlockSpec(memory_space=space) for space in in_spaces],
        out_specs=[pl.BlockSpec(memory_space=pltpu.VMEM)] * len(outs),
        scratch_shapes=list(scratch)
        + [pltpu.SemaphoreType.DMA((copies,)), pltpu.SemaphoreType.DMA((copies,))],
        compiler_params=pltpu.CompilerParams(
            collective_id=ident, has_side_effects=True, vmem_limit_bytes=60 * 2**20
        ),
        name=name,
    )(*args)


def gather_body(features, out, send, recv):
    me, wire = Place(), Wire(send, recv)
    right, left = me.along("x", 1), me.along("x", -1)
    mate = me.at(y=me.high * 2 + 1 - me.low)
    enter([mate, right, left])
    row = me.row
    first = wire.push(features, out.at[row], mate)
    own = [wire.push(features, out.at[row], device) for device in (right, left)]
    out[row] = features[...]
    wire.arrived(first)
    row_mate = me.x * 2 + 1 - me.low
    other = [wire.push(out.at[row_mate], out.at[row_mate], device) for device in (right, left)]
    for pair, low in ((own, me.low), (other, 1 - me.low)):
        for side, rows in enumerate(halves(TILE)):
            wire.arrived(pair[side])
            held = ((me.x + (3 if side == 0 else 1)) % 4) * 2 + low
            wire.push(out.at[held, rows], out.at[held, rows], (right, left)[side])
    wire.finish()


def contract(a, b, left, right):
    return lax.dot_general(a, b, (((left,), (right,)), ((), ())), preferred_element_type=F32)


OFFSETS = (4, 3, 5, 2, 6, 1, 7, 0)


def dense_body(
    totals, cot, kinds, table, w_in, w_out,
    mixed, gathered, w_part, g_part,
    own, sib, z_out, z_in, y_out, y_in, mine, grad_act, gains,
    scaled2, act_half, act2, hid_half, hid2, cot2,
    weights, x_out, x_in, summed, v_out, v_in, g_out, g_in,
    local, send, recv,
):
    me, wire = Place(), Wire(send, recv)
    twin = me.at(core=1 - me.core)
    across = me.along("y", 2)
    z_side = (me.along("z", 1), me.along("z", -1))
    x_side = (me.along("x", 1), me.along("x", -1))
    y_side = (me.along("y", 1), me.along("y", -1))
    enter([twin, across, *z_side, *x_side, *y_side])

    loads, parts = {}, {}
    for order, offset in enumerate(OFFSETS):
        for side in range(2):
            slot = order * 2 + side
            tile = ((me.high + 1 + side) % 2) * 16 + ((me.z + offset) % 8) * 2
            load = pltpu.make_async_copy(totals.at[tile + me.core], own.at[slot], local.at[slot])
            load.start()
            loads[slot] = load
            parts[slot] = wire.push(totals.at[tile + 1 - me.core], sib.at[slot], twin)
    cot_sent = wire.push(cot, cot2.at[pl.ds(TILE, TILE)], twin)
    cot2[0:TILE] = cot[...]
    grad_act[...] = contract(cot[...], w_out[...], 1, 1)
    kind = kinds[...]
    chosen = jnp.zeros((TILE, F), F32)
    for t in range(TYPES):
        chosen = jnp.where(kind == t, table[t : t + 1], chosen)
    gains[...] = chosen

    def base(offset, side):
        slot = OFFSETS.index(offset) * 2 + side
        if slot in loads:
            loads.pop(slot).wait()
            wire.arrived(parts[slot])
        return slot

    sent = {}
    for hop in (4, 3, 2, 1):
        for side in range(2):
            for turn in range(2):
                offset = hop if turn == 0 else 8 - hop
                slot = base(offset, side)
                stage = z_out.at[turn, side, hop - 1]
                for part, rows in enumerate(halves(TILE)):
                    if hop == 4 and part != turn:
                        continue
                    value = own[slot, rows] + sib[slot, rows]
                    if hop < 3 or (hop == 3 and part == turn):
                        wire.arrived(sent[turn, side, hop + 1])
                        value = value + z_in[turn, side, hop, rows].astype(F32)
                    stage[rows] = value.astype(BF)
                moved = halves(TILE)[turn] if hop == 4 else pl.ds(0, TILE)
                sent[turn, side, hop] = wire.push(
                    z_out.at[turn, side, hop - 1, moved],
                    z_in.at[turn, side, hop - 1, moved],
                    z_side[turn],
                )
    ends = []
    for side in range(2):
        slot = base(0, side)
        value = own[slot] + sib[slot]
        for turn in range(2):
            wire.arrived(sent[turn, side, 1])
            value = value + z_in[turn, side, 0].astype(F32)
        if side == 0:
            y_out[...] = value.astype(BF)
            crossed = wire.push(y_out, y_in, across)
        else:
            ends.append(value)
    wire.arrived(crossed)
    aggregate = ends[0] + y_in[...].astype(F32)

    center = jnp.mean(aggregate, axis=-1, keepdims=True)
    spread = jnp.mean(jnp.square(aggregate - center), axis=-1, keepdims=True)
    inverse = lax.rsqrt(spread + 1e-05)
    normed = (aggregate - center) * inverse
    scaled = (normed * gains[...]).astype(BF)
    scaled2[0:TILE] = scaled
    scaled_sent = wire.push(scaled2.at[pl.ds(0, TILE)], scaled2.at[pl.ds(TILE, TILE)], twin)
    hidden = contract(scaled, w_in[...], 1, 0)
    sigmoid = jax.nn.sigmoid(hidden)
    activated = (hidden * sigmoid).astype(BF)
    grad_hidden = (grad_act[...] * sigmoid * (1.0 + hidden * (1.0 - sigmoid))).astype(BF)
    grad_scaled = contract(grad_hidden, w_in[...], 1, 1)
    grad_normed = grad_scaled * gains[...]
    grad_rows = (
        cot[...].astype(F32)
        + inverse
        * (
            grad_normed
            - jnp.mean(grad_normed, axis=-1, keepdims=True)
            - normed * jnp.mean(grad_normed * normed, axis=-1, keepdims=True)
        )
    ).astype(BF)
    mine[...] = grad_rows
    col = me.col
    crossed = wire.push(mine, gathered.at[col], across)
    own_sent = [wire.push(mine, gathered.at[col], device) for device in z_side]
    wire.push(mine, gathered.at[col], twin)
    gathered[col] = grad_rows
    for half in range(2):
        act_half[half] = activated[:, half * F : (half + 1) * F]
        hid_half[half] = grad_hidden[:, half * F : (half + 1) * F]
    late = pl.ds(TILE, TILE)
    act_sent = wire.push(act_half.at[1 - me.core], act2.at[late], twin)
    hid_sent = wire.push(hid_half.at[1 - me.core], hid2.at[late], twin)
    act2[0:TILE] = act_half[me.core]
    hid2[0:TILE] = hid_half[me.core]
    product = grad_scaled * normed
    for t in range(TYPES):
        g_out[0, t : t + 1] = jnp.sum(jnp.where(kind == t, product, 0.0), axis=0, keepdims=True)
    gain_sent = wire.push(g_out.at[0], g_in.at[0], twin)

    def index_of(family, offset):
        high = me.high if family == 0 else 1 - me.high
        return high * 16 + ((me.z + offset + 8) % 8) * 2 + me.core

    wire.arrived(crossed)
    place = index_of(1, 0)
    other_sent = [
        wire.push(gathered.at[place], gathered.at[place], device) for device in z_side
    ]
    wire.push(gathered.at[place], gathered.at[place], twin)
    mixed[...] = (aggregate + contract(activated, w_out[...], 1, 0)).astype(BF)
    flows = [own_sent, other_sent]

    def forward(hop):
        for family in range(2):
            for turn in range(2):
                wire.arrived(flows[family][turn])
                place = index_of(family, (1 - hop) if turn == 0 else (hop - 1))
                moved = halves(TILE)[turn] if hop == 4 else pl.ds(0, TILE)
                flows[family][turn] = wire.push(
                    gathered.at[place, moved], gathered.at[place, moved], z_side[turn]
                )
                wire.push(gathered.at[place], gathered.at[place], twin)

    forward(2)

    for arrival in (cot_sent, scaled_sent, act_sent, hid_sent, gain_sent):
        wire.arrived(arrival)
    for part in range(4):
        columns = slice((part % 2) * 256, (part % 2) * 256 + 256)
        if part < 2:
            weights[part] = contract(act2[:, columns], cot2[...], 0, 0)
        else:
            weights[part] = contract(scaled2[:, columns], hid2[...], 0, 0)

    def gain_step(phase, device):
        g_out[phase] = g_out[phase - 1] + g_in[phase - 1]
        return wire.push(g_out.at[phase], g_in.at[phase], device)

    gain_sent = gain_step(1, me.at(x=me.x + 1 - 2 * (me.x % 2)))
    ring = []
    quarter = halves(256)
    far = (me.x + 2) % 4
    for turn in range(2):
        x_out[turn, 1, quarter[turn]] = weights[far, quarter[turn]].astype(BF)
        ring.append(
            wire.push(
                x_out.at[turn, 1, quarter[turn]], x_in.at[turn, 1, quarter[turn]], x_side[turn]
            )
        )
    forward(3)
    wire.arrived(gain_sent)
    gain_sent = gain_step(2, me.at(x=3 - me.x))
    for turn in range(2):
        wire.arrived(ring[turn])
        near = (me.x + (1 if turn == 0 else 3)) % 4
        x_out[turn, 0, quarter[1 - turn]] = weights[near, quarter[1 - turn]].astype(BF)
        x_out[turn, 0, quarter[turn]] = (
            weights[near, quarter[turn]] + x_in[turn, 1, quarter[turn]].astype(F32)
        ).astype(BF)
        ring[turn] = wire.push(x_out.at[turn, 0], x_in.at[turn, 0], x_side[turn])
    forward(4)
    wire.arrived(gain_sent)
    gain_sent = gain_step(3, me.at(y=me.y + 1 - 2 * (me.y % 2)))
    for turn in range(2):
        wire.arrived(ring[turn])
    for part in range(4):
        rows = pl.ds(part * 64, 64)
        summed[part] = (
            weights[me.x, rows] + x_in[0, 0, rows].astype(F32) + x_in[1, 0, rows].astype(F32)
        )
    eighth = halves(64)
    far = (me.y + 2) % 4
    for turn in range(2):
        v_out[turn, 1, eighth[turn]] = summed[far, eighth[turn]]
        ring[turn] = wire.push(
            v_out.at[turn, 1, eighth[turn]], v_in.at[turn, 1, eighth[turn]], y_side[turn]
        )
    wire.arrived(gain_sent)
    gain_sent = gain_step(4, me.at(y=3 - me.y))
    for turn in range(2):
        wire.arrived(ring[turn])
        near = (me.y + (1 if turn == 0 else 3)) % 4
        v_out[turn, 0, eighth[1 - turn]] = summed[near, eighth[1 - turn]]
        v_out[turn, 0, eighth[turn]] = summed[near, eighth[turn]] + v_in[turn, 1, eighth[turn]]
        ring[turn] = wire.push(v_out.at[turn, 0], v_in.at[turn, 0], y_side[turn])
    for family in range(2):
        for turn in range(2):
            wire.arrived(flows[family][turn])
        place = index_of(family, 4)
        wire.push(gathered.at[place], gathered.at[place], twin)
    for turn in range(2):
        wire.arrived(ring[turn])
    for part in range(8):
        rows = pl.ds(part * 8, 8)
        w_part[part] = summed[me.y, rows] + v_in[0, 0, rows] + v_in[1, 0, rows]
    wire.arrived(gain_sent)
    g_part[...] = g_out[4] + g_in[4]
    wire.finish()


def finish_body(
    factor, back, w_part, g_part, grad_x, w_all, gain,
    z_in, x_out, x_in, y_out, y_in, piece, g_out, g_in, send, recv,
):
    me, wire = Place(), Wire(send, recv)
    twin = me.at(core=1 - me.core)
    z_all = [me.along("z", step) for step in range(1, 8)]
    x_side = (me.along("x", 1), me.along("x", -1))
    y_side = (me.along("y", 1), me.along("y", -1))
    mate = me.at(y=me.high * 2 + 1 - me.low)
    enter([twin, *z_all, *x_side, *y_side])

    scattered = [
        wire.push(w_part.at[(me.z + step) % 8], z_in.at[step - 1], z_all[step - 1])
        for step in range(1, 8)
    ]
    gain_sent = wire.push(g_part, g_in.at[0], me.at(z=me.z + 1 - 2 * (me.z % 2)))
    ring = {}
    for side in range(2):
        low = (me.low + 1 + side) % 2
        far = ((me.x + 2) % 4) * 2 + low
        for turn, rows in enumerate(halves(TILE)):
            x_out[turn, side, 1, rows] = back[far, rows].astype(BF)
            ring[turn, side] = wire.push(
                x_out.at[turn, side, 1, rows], x_in.at[turn, side, 1, rows], x_side[turn]
            )
    total = w_part[me.z]
    for step in range(7):
        wire.arrived(scattered[step])
        total = total + z_in[step]
    total = (total * factor).astype(BF)
    piece[...] = total
    w_all[me.core, me.x, me.y, me.z] = total
    spot = w_all.at[me.core, me.x, me.y, me.z]
    spread = [wire.push(piece, spot, device) for device in z_all]
    wire.arrived(gain_sent)
    base = (me.z // 4) * 4
    g_out[0] = g_part[...] + g_in[0]
    gain_sent = wire.push(g_out.at[0], g_in.at[1], me.at(z=base + 3 - me.z % 4))
    for side in range(2):
        low = (me.low + 1 + side) % 2
        for turn, rows in enumerate(halves(TILE)):
            wire.arrived(ring[turn, side])
            near = ((me.x + (1 if turn == 0 else 3)) % 4) * 2 + low
            rest = halves(TILE)[1 - turn]
            x_out[turn, side, 0, rest] = back[near, rest].astype(BF)
            x_out[turn, side, 0, rows] = (
                back[near, rows] + x_in[turn, side, 1, rows].astype(F32)
            ).astype(BF)
            ring[turn, side] = wire.push(
                x_out.at[turn, side, 0], x_in.at[turn, side, 0], x_side[turn]
            )
    wire.arrived(gain_sent)
    g_out[1] = g_out[0] + g_in[1]
    gain_sent = wire.push(g_out.at[1], g_in.at[2], me.at(z=(me.z + 4) % 8))
    for index in spread:
        wire.arrived(index)
    core = me.core
    block = w_all.at[core, me.x, me.y]
    column = [wire.push(block, block, device) for device in y_side]
    ends = []
    for side in range(2):
        low = (me.low + 1 + side) % 2
        value = back[me.x * 2 + low]
        for turn in range(2):
            wire.arrived(ring[turn, side])
            value = value + x_in[turn, side, 0].astype(F32)
        if side == 0:
            y_out[...] = value.astype(BF)
            crossed = wire.push(y_out, y_in, mate)
        else:
            ends.append(value)
    for turn, rows in enumerate((pl.ds(0, 4), pl.ds(4, 4))):
        wire.arrived(column[turn])
        held = (me.y + (3 if turn == 0 else 1)) % 4
        view = w_all.at[core, me.x, held, rows]
        column[turn] = wire.push(view, view, y_side[turn])
    for turn in range(2):
        wire.arrived(column[turn])
    block = w_all.at[core, me.x]
    plane = [wire.push(block, block, device) for device in x_side]
    wire.push(block, block, twin)
    wire.arrived(crossed)
    grad_x[...] = ends[0] + y_in[...].astype(F32)
    wire.arrived(gain_sent)
    gain[...] = (g_out[1] + g_in[2]) * factor
    for turn, rows in enumerate((pl.ds(0, 2), pl.ds(2, 2))):
        wire.arrived(plane[turn])
        held = (me.x + (3 if turn == 0 else 1)) % 4
        view = w_all.at[core, held, rows]
        plane[turn] = wire.push(view, view, x_side[turn])
        block = w_all.at[core, held]
        wire.push(block, block, twin)
    for turn in range(2):
        wire.arrived(plane[turn])
    block = w_all.at[core, (me.x + 2) % 4]
    wire.push(block, block, twin)
    wire.finish()


def shards(
    features,
    tile_vals,
    tile_row,
    tile_col,
    tile_count,
    node_type,
    type_gain,
    w_in,
    w_out,
    cotangent,
):
    row_count = lax.axis_size("row")
    col_count = lax.axis_size("col")
    hid = w_in.shape[1]
    total_nodes = TILE * row_count * col_count
    factor = float(total_nodes) ** (-0.5)
    weights_all, row_ids, col_ids = tile_vals[0], tile_row[0], tile_col[0]
    live_count = tile_count[0]
    shape = jax.ShapeDtypeStruct
    vmem = pltpu.VMEM
    (gathered,) = remote_call(
        gather_body, "gather_features", 1,
        [shape((row_count, TILE, F), BF)], [vmem], [], 9, (features,),
    )
    totals = sweep(weights_all, row_ids, col_ids, live_count, gathered, col_count, True, F32)
    mixed, grad_sources, w_part, g_part = remote_call(
        dense_body, "dense", 2,
        [
            shape((TILE, F), BF),
            shape((col_count, TILE, F), BF),
            shape((8, 8, F), F32),
            shape((TYPES, F), F32),
        ],
        [pl.ANY] + [vmem] * 5,
        [
            vmem((16, TILE, F), F32), vmem((16, TILE, F), F32),
            vmem((2, 2, 4, TILE, F), BF), vmem((2, 2, 4, TILE, F), BF),
            vmem((TILE, F), BF), vmem((TILE, F), BF), vmem((TILE, F), BF),
            vmem((TILE, hid), F32), vmem((TILE, F), F32),
            vmem((2 * TILE, F), BF), vmem((2, TILE, F), BF), vmem((2 * TILE, F), BF),
            vmem((2, TILE, F), BF), vmem((2 * TILE, F), BF), vmem((2 * TILE, F), BF),
            vmem((4, 256, F), F32), vmem((2, 2, 256, F), BF), vmem((2, 2, 256, F), BF),
            vmem((4, 64, F), F32), vmem((2, 2, 64, F), F32), vmem((2, 2, 64, F), F32),
            vmem((5, TYPES, F), F32), vmem((5, TYPES, F), F32),
            pltpu.SemaphoreType.DMA((16,)),
        ],
        96,
        (totals, cotangent, node_type[:, None], type_gain, w_in, w_out),
    )
    back = sweep(weights_all, row_ids, col_ids, live_count, grad_sources, row_count, False, F32)
    grad_x, w_all, gain = remote_call(
        functools.partial(finish_body, factor), "finish", 3,
        [
            shape((TILE, F), F32),
            shape((2, 4, 4, 8, 8, F), BF),
            shape((TYPES, F), F32),
        ],
        [vmem] * 3,
        [
            vmem((7, 8, F), F32),
            vmem((2, 2, 2, TILE, F), BF), vmem((2, 2, 2, TILE, F), BF),
            vmem((TILE, F), BF), vmem((TILE, F), BF), vmem((8, F), BF),
            vmem((2, TYPES, F), F32), vmem((3, TYPES, F), F32),
        ],
        48,
        (back, w_part, g_part),
    )
    w_all = w_all.reshape(2, 2, 512, F).astype(F32)
    grad_w_out = w_all[:, 0].reshape(hid, F)
    grad_w_in = jnp.concatenate([w_all[0, 1], w_all[1, 1]], axis=1)
    return (mixed, grad_x, grad_w_in, grad_w_out, gain)


def solution(mesh):
    return jax.shard_map(
        shards,
        mesh=mesh,
        in_specs=(
            P(("col", "row"), None),
            P("row", "col", None, None),
            P("row", "col"),
            P("row", "col"),
            P("row", "col"),
            P(("row", "col")),
            P(),
            P(),
            P(),
            P(("row", "col"), None),
        ),
        out_specs=(P(("row", "col"), None), P(("col", "row"), None), P(), P(), P()),
        check_vma=False,
    )
```

```python
import functools

import jax
import jax.numpy as jnp
from jax import lax
from jax.experimental import pallas as pl
from jax.experimental.pallas import tpu as pltpu
from jax.sharding import PartitionSpec as P

F = 512
TYPES = 8
TILE = 128
GROUP = 16
UNROLL = 4
PHASES = 8
MESH = pl.DeviceIdType.MESH
BF = jnp.bfloat16
F32 = jnp.float32
OFFSETS = (4, 3, 5, 2, 6, 1, 7, 0)


def build_body(count, rows, cols, weights, out, acc):
    step = pl.program_id(0)

    @pl.when(step == 0)
    def _():
        acc[...] = jnp.zeros_like(acc)

    first = step * GROUP
    rounds = jnp.clip((count[0] - first + UNROLL - 1) // UNROLL, 0, GROUP // UNROLL)

    @pl.when(step < PHASES)
    def _():
        def advance(block, carry):
            for u in range(UNROLL):
                inner = block * UNROLL + u
                slot = first + inner
                place = jnp.where(slot < count[0], rows[slot], acc.shape[0] - 1)
                lanes = pl.ds(pl.multiple_of(cols[slot] * TILE, TILE), TILE)
                acc[place, :, lanes] += weights[inner].astype(F32)
            return carry

        lax.fori_loop(0, rounds, advance, 0)

    @pl.when(step >= PHASES)
    def _():
        for part in range(out.shape[0]):
            out[part] = acc[(step - PHASES) * out.shape[0] + part].astype(BF)


def build(weights_all, row_ids, col_ids, live_count, tall, wide):
    last = lambda count: (count[0] - 1) // GROUP
    return pl.pallas_call(
        build_body,
        grid_spec=pltpu.PrefetchScalarGridSpec(
            num_scalar_prefetch=3,
            grid=(2 * PHASES,),
            in_specs=[
                pl.BlockSpec(
                    (GROUP, TILE, TILE), lambda i, n, r, c: (jnp.minimum(i, last(n)), 0, 0)
                ),
            ],
            out_specs=pl.BlockSpec(
                (tall // PHASES, TILE, wide), lambda i, n, r, c: (jnp.maximum(i - PHASES, 0), 0, 0)
            ),
            scratch_shapes=[pltpu.VMEM((tall + 1, TILE, wide), F32)],
        ),
        out_shape=jax.ShapeDtypeStruct((tall, TILE, wide), BF),
        name="build_block",
    )(live_count, row_ids, col_ids, weights_all)


class Place:
    def __init__(self):
        row = lax.axis_index("row")
        col = lax.axis_index("col")
        self.row, self.col = row, col
        self.x, self.low = row // 2, row % 2
        self.high, self.z, self.core = col // 16, (col // 2) % 8, col % 2
        self.y = self.high * 2 + self.low

    def at(self, x=None, y=None, z=None, core=None):
        x = self.x if x is None else x
        y = self.y if y is None else y
        z = self.z if z is None else z
        core = self.core if core is None else core
        return (x * 2 + y % 2, (y // 2) * 16 + z * 2 + core)

    def along(self, axis, offset):
        size = {"x": 4, "y": 4, "z": 8}[axis]
        return self.at(**{axis: (getattr(self, axis) + offset + size) % size})


class Wire:
    def __init__(self, send, recv):
        self.send, self.recv, self.copies = send, recv, []

    def push(self, source, target, device):
        index = len(self.copies)
        copy = pltpu.make_async_remote_copy(
            src_ref=source,
            dst_ref=target,
            send_sem=self.send.at[index],
            recv_sem=self.recv.at[index],
            device_id=device,
            device_id_type=MESH,
        )
        copy.start()
        self.copies.append([copy, False])
        return index

    def arrived(self, index):
        if not self.copies[index][1]:
            self.copies[index][0].wait_recv()
            self.copies[index][1] = True

    def finish(self):
        for index, (copy, _) in enumerate(self.copies):
            self.arrived(index)
            copy.wait_send()


def enter(devices):
    barrier = pltpu.get_barrier_semaphore()
    for device in devices:
        pl.semaphore_signal(barrier, inc=1, device_id=device, device_id_type=MESH)
    pl.semaphore_wait(barrier, len(devices))


def halves(size):
    return (pl.ds(0, size // 2), pl.ds(size // 2, size // 2))


def contract(a, b, left, right):
    return lax.dot_general(a, b, (((left,), (right,)), ((), ())), preferred_element_type=F32)


def layer_body(
    factor,
    features, adjacency, cot, kinds, table, w_in, w_out,
    mixed, grad_x, w_all, gain,
    sources, blocks, own, sib_out, sib_in, z_out, z_in, y_out, y_in,
    mine, gathered, back, grad_act, gains,
    scaled2, act_half, act2, hid_half, hid2, cot2,
    weights, x_out, x_in, summed, v_out, v_in, w_part, w_in_z, piece, g_out, g_in,
    b_out, b_in, c_out, c_in,
    local, send, recv,
):
    me, wire = Place(), Wire(send, recv)
    twin = me.at(core=1 - me.core)
    across = me.along("y", 2)
    mate = me.at(y=me.high * 2 + 1 - me.low)
    z_side = (me.along("z", 1), me.along("z", -1))
    x_side = (me.along("x", 1), me.along("x", -1))
    y_side = (me.along("y", 1), me.along("y", -1))
    z_all = [me.along("z", step) for step in range(1, 8)]
    whole = pl.ds(0, TILE)

    loads = []
    for order, offset in enumerate(OFFSETS):
        group = []
        for part in range(4):
            which, side = part // 2, part % 2
            high = (me.high + 1 + side) % 2
            core = me.core if which == 0 else 1 - me.core
            tile = high * 16 + ((me.z + offset) % 8) * 2 + core
            copy = pltpu.make_async_copy(
                adjacency.at[tile],
                blocks.at[order, pl.ds(part * TILE, TILE)],
                local.at[order * 4 + part],
            )
            copy.start()
            group.append(copy)
        loads.append(group)

    enter([twin, across, *z_side, *x_side, *y_side])

    row = me.row
    first = wire.push(features, sources.at[row], mate)
    direct = [wire.push(features, sources.at[row], device) for device in x_side]
    cot_sent = wire.push(cot, cot2.at[pl.ds(TILE, TILE)], twin)
    sources[row] = features[...]
    wire.arrived(first)
    row_mate = me.x * 2 + 1 - me.low
    other = [wire.push(sources.at[row_mate], sources.at[row_mate], device) for device in x_side]
    cot2[0:TILE] = cot[...]
    grad_act[...] = contract(cot[...], w_out[...], 1, 1)
    kind = jnp.transpose(jnp.broadcast_to(kinds[...].astype(F32), (TILE, TILE)))[:, :1]
    chosen = jnp.zeros((TILE, F), F32)
    for t in range(TYPES):
        chosen = jnp.where(kind == float(t), table[t : t + 1], chosen)
    gains[...] = chosen
    for pair, low in ((direct, me.low), (other, 1 - me.low)):
        for turn, rows in enumerate(halves(TILE)):
            wire.arrived(pair[turn])
            held = ((me.x + (3 if turn == 0 else 1)) % 4) * 2 + low
            view = sources.at[held, rows]
            pair[turn] = wire.push(view, view, x_side[turn])
    for pair in (direct, other):
        for turn in range(2):
            wire.arrived(pair[turn])

    parts = {}

    def multiply(order):
        for copy in loads[order]:
            copy.wait()
        value = sources[...].reshape(sources.shape[0] * TILE, F)
        sib_out[order] = contract(blocks[order, 256:512], value, 1, 0)
        parts[order] = wire.push(sib_out.at[order], sib_in.at[order], twin)
        own[order] = contract(blocks[order, 0:256], value, 1, 0)

    sent = {}

    def reduce_hop(hop):
        for side in range(2):
            for turn in range(2):
                order = OFFSETS.index(hop if turn == 0 else 8 - hop)
                wire.arrived(parts[order])
                for part in range(2):
                    if hop == 4 and part != turn:
                        continue
                    rows = pl.ds(part * 64, 64)
                    base = pl.ds(side * TILE + part * 64, 64)
                    value = own[order, base] + sib_in[order, base]
                    if hop < 3 or (hop == 3 and part == turn):
                        wire.arrived(sent[turn, side, hop + 1])
                        value = value + z_in[turn, side, hop, rows].astype(F32)
                    z_out[turn, side, hop - 1, rows] = value.astype(BF)
                moved = pl.ds(turn * 64, 64) if hop == 4 else whole
                sent[turn, side, hop] = wire.push(
                    z_out.at[turn, side, hop - 1, moved],
                    z_in.at[turn, side, hop - 1, moved],
                    z_side[turn],
                )

    multiply(0)
    multiply(1)
    reduce_hop(4)
    multiply(2)
    reduce_hop(3)
    multiply(3)
    multiply(4)
    reduce_hop(2)
    multiply(5)
    multiply(6)
    reduce_hop(1)
    multiply(7)
    wire.arrived(parts[7])
    ends = []
    for side in range(2):
        rows = pl.ds(side * TILE, TILE)
        value = own[7, rows] + sib_in[7, rows]
        for turn in range(2):
            wire.arrived(sent[turn, side, 1])
            value = value + z_in[turn, side, 0].astype(F32)
        if side == 0:
            y_out[...] = value.astype(BF)
            crossed = wire.push(y_out, y_in, across)
        else:
            ends.append(value)
    wire.arrived(crossed)
    aggregate = ends[0] + y_in[...].astype(F32)

    center = jnp.mean(aggregate, axis=-1, keepdims=True)
    spread = jnp.mean(jnp.square(aggregate - center), axis=-1, keepdims=True)
    inverse = lax.rsqrt(spread + 1e-05)
    normed = (aggregate - center) * inverse
    scaled = (normed * gains[...]).astype(BF)
    scaled2[0:TILE] = scaled
    late = pl.ds(TILE, TILE)
    scaled_sent = wire.push(scaled2.at[whole], scaled2.at[late], twin)
    hidden = contract(scaled, w_in[...], 1, 0)
    sigmoid = jax.nn.sigmoid(hidden)
    activated = (hidden * sigmoid).astype(BF)
    grad_hidden = (grad_act[...] * sigmoid * (1.0 + hidden * (1.0 - sigmoid))).astype(BF)
    grad_scaled = contract(grad_hidden, w_in[...], 1, 1)
    grad_normed = grad_scaled * gains[...]
    grad_rows = cot[...].astype(F32) + inverse * (
        grad_normed
        - jnp.mean(grad_normed, axis=-1, keepdims=True)
        - normed * jnp.mean(grad_normed * normed, axis=-1, keepdims=True)
    )
    turned = jnp.transpose(grad_rows).astype(BF)
    mine[...] = turned
    col = me.col
    crossed = wire.push(mine, gathered.at[col], across)
    own_sent = [wire.push(mine, gathered.at[col], device) for device in z_side]
    shared = {(0, 0): wire.push(mine, gathered.at[col], twin)}
    gathered[col] = turned
    for half in range(2):
        act_half[half] = activated[:, half * F : (half + 1) * F]
        hid_half[half] = grad_hidden[:, half * F : (half + 1) * F]
    act_sent = wire.push(act_half.at[1 - me.core], act2.at[late], twin)
    hid_sent = wire.push(hid_half.at[1 - me.core], hid2.at[late], twin)
    act2[0:TILE] = act_half[me.core]
    hid2[0:TILE] = hid_half[me.core]
    product = grad_scaled * normed
    for t in range(TYPES):
        g_out[0, t : t + 1] = jnp.sum(
            jnp.where(kind == float(t), product, 0.0), axis=0, keepdims=True
        )
    tally = {"sent": wire.push(g_out.at[0], g_in.at[0], twin), "phase": 0}

    def gain_step(device):
        phase = tally["phase"]
        wire.arrived(tally["sent"])
        g_out[phase + 1] = g_out[phase] + g_in[phase]
        tally["sent"] = wire.push(g_out.at[phase + 1], g_in.at[phase + 1], device)
        tally["phase"] = phase + 1

    def index_of(family, offset, core):
        high = me.high if family == 0 else 1 - me.high
        return high * 16 + ((me.z + offset + 8) % 8) * 2 + core

    flows = [own_sent, None]

    def forward(hop, family):
        for turn in range(2):
            wire.arrived(flows[family][turn])
            offset = 1 - hop if turn == 0 else hop - 1
            place = index_of(family, offset, me.core)
            moved = halves(F)[turn] if hop == 4 else pl.ds(0, F)
            view = gathered.at[place, moved]
            flows[family][turn] = wire.push(view, view, z_side[turn])
            view = gathered.at[place]
            shared[family, offset % 8] = wire.push(view, view, twin)

    def pull(offset):
        order = OFFSETS.index(offset)
        pieces = []
        for part in range(4):
            which, side = part // 2, part % 2
            if which == 1:
                wire.arrived(shared[1 - side, offset])
            core = me.core if which == 0 else 1 - me.core
            pieces.append(gathered[index_of(1 - side, offset, core)])
        value = contract(jnp.concatenate(pieces, axis=1), blocks[order], 1, 0)
        for part in range(8):
            piece_of = value[:, part * TILE : (part + 1) * TILE]
            back[part] = piece_of if offset == 0 else back[part] + piece_of

    ring = {}

    def weight_start():
        for arrival in (cot_sent, scaled_sent, act_sent, hid_sent):
            wire.arrived(arrival)
        far = (me.x + 2) % 4
        for part in range(4):
            columns = slice((part % 2) * 256, (part % 2) * 256 + 256)
            if part < 2:
                weights[part] = contract(act2[:, columns], cot2[...], 0, 0)
            else:
                weights[part] = contract(scaled2[:, columns], hid2[...], 0, 0)
        for turn, rows in enumerate(halves(256)):
            x_out[turn, 1, rows] = weights[far, rows].astype(BF)
            ring[turn] = wire.push(x_out.at[turn, 1, rows], x_in.at[turn, 1, rows], x_side[turn])

    def weight_x():
        for turn, rows in enumerate(halves(256)):
            rest = halves(256)[1 - turn]
            near = (me.x + (1 if turn == 0 else 3)) % 4
            wire.arrived(ring[turn])
            x_out[turn, 0, rest] = weights[near, rest].astype(BF)
            x_out[turn, 0, rows] = (
                weights[near, rows] + x_in[turn, 1, rows].astype(F32)
            ).astype(BF)
            ring[turn] = wire.push(x_out.at[turn, 0], x_in.at[turn, 0], x_side[turn])

    def weight_y_start():
        for turn in range(2):
            wire.arrived(ring[turn])
        for part in range(4):
            rows = pl.ds(part * 64, 64)
            summed[part] = (
                weights[me.x, rows] + x_in[0, 0, rows].astype(F32) + x_in[1, 0, rows].astype(F32)
            )
        far = (me.y + 2) % 4
        for turn, rows in enumerate(halves(64)):
            v_out[turn, 1, rows] = summed[far, rows]
            ring[turn] = wire.push(v_out.at[turn, 1, rows], v_in.at[turn, 1, rows], y_side[turn])

    def weight_y():
        for turn, rows in enumerate(halves(64)):
            rest = halves(64)[1 - turn]
            near = (me.y + (1 if turn == 0 else 3)) % 4
            wire.arrived(ring[turn])
            v_out[turn, 0, rest] = summed[near, rest]
            v_out[turn, 0, rows] = summed[near, rows] + v_in[turn, 1, rows]
            ring[turn] = wire.push(v_out.at[turn, 0], v_in.at[turn, 0], y_side[turn])

    def weight_z_start():
        for turn in range(2):
            wire.arrived(ring[turn])
        for part in range(8):
            rows = pl.ds(part * 8, 8)
            w_part[part] = summed[me.y, rows] + v_in[0, 0, rows] + v_in[1, 0, rows]
        ring["z"] = [
            wire.push(w_part.at[(me.z + step) % 8], w_in_z.at[step - 1], z_all[step - 1])
            for step in range(1, 8)
        ]

    def weight_z():
        total = w_part[me.z]
        for step in range(7):
            wire.arrived(ring["z"][step])
            total = total + w_in_z[step]
        total = (total * factor).astype(BF)
        piece[...] = total
        w_all[me.core, me.x, me.y, me.z] = total
        spot = w_all.at[me.core, me.x, me.y, me.z]
        ring["z"] = [wire.push(piece, spot, device) for device in z_all]

    def spread_y():
        for index in ring["z"]:
            wire.arrived(index)
        view = w_all.at[me.core, me.x, me.y]
        ring["y"] = [wire.push(view, view, device) for device in y_side]

    def spread_y_far():
        for turn in range(2):
            wire.arrived(ring["y"][turn])
            held = (me.y + (3 if turn == 0 else 1)) % 4
            view = w_all.at[me.core, me.x, held, pl.ds(turn * 4, 4)]
            ring["y"][turn] = wire.push(view, view, y_side[turn])

    def spread_x():
        for turn in range(2):
            wire.arrived(ring["y"][turn])
        view = w_all.at[me.core, me.x]
        ring["x"] = [wire.push(view, view, device) for device in x_side]
        wire.push(view, view, twin)

    def spread_x_far():
        for turn in range(2):
            wire.arrived(ring["x"][turn])
            held = (me.x + (3 if turn == 0 else 1)) % 4
            view = w_all.at[me.core, held, pl.ds(turn * 2, 2)]
            ring["x"][turn] = wire.push(view, view, x_side[turn])
            view = w_all.at[me.core, held]
            wire.push(view, view, twin)

    wire.arrived(crossed)
    place = index_of(1, 0, me.core)
    view = gathered.at[place]
    flows[1] = [wire.push(view, view, device) for device in z_side]
    shared[1, 0] = wire.push(view, view, twin)
    mixed[...] = (aggregate + contract(activated, w_out[...], 1, 0)).astype(BF)
    forward(2, 0)
    weight_start()
    forward(2, 1)
    gain_step(me.at(x=me.x + 1 - 2 * (me.x % 2)))
    pull(0)
    forward(3, 0)
    pull(7)
    forward(3, 1)
    weight_x()
    gain_step(me.at(x=3 - me.x))
    pull(1)
    forward(4, 0)
    pull(6)
    forward(4, 1)
    weight_y_start()
    gain_step(me.at(y=me.y + 1 - 2 * (me.y % 2)))
    pull(2)
    weight_y()
    gain_step(me.at(y=3 - me.y))
    for family in range(2):
        for turn in range(2):
            wire.arrived(flows[family][turn])
        view = gathered.at[index_of(family, 4, me.core)]
        shared[family, 4] = wire.push(view, view, twin)
    pull(5)
    weight_z_start()
    gain_step(me.at(z=me.z + 1 - 2 * (me.z % 2)))
    pull(3)
    pull(4)

    flow = {}
    for side in range(2):
        low = (me.low + 1 + side) % 2
        far = ((me.x + 2) % 4) * 2 + low
        for turn, rows in enumerate(halves(F)):
            b_out[turn, side, 1, rows] = back[far, rows].astype(BF)
            flow[turn, side] = wire.push(
                b_out.at[turn, side, 1, rows], b_in.at[turn, side, 1, rows], x_side[turn]
            )
    weight_z()
    gain_step(me.at(z=(me.z // 4) * 4 + 3 - me.z % 4))
    for side in range(2):
        low = (me.low + 1 + side) % 2
        for turn, rows in enumerate(halves(F)):
            wire.arrived(flow[turn, side])
            near = ((me.x + (1 if turn == 0 else 3)) % 4) * 2 + low
            rest = halves(F)[1 - turn]
            b_out[turn, side, 0, rest] = back[near, rest].astype(BF)
            b_out[turn, side, 0, rows] = (
                back[near, rows] + b_in[turn, side, 1, rows].astype(F32)
            ).astype(BF)
            flow[turn, side] = wire.push(
                b_out.at[turn, side, 0], b_in.at[turn, side, 0], x_side[turn]
            )
    spread_y()
    gain_step(me.at(z=(me.z + 4) % 8))
    spread_y_far()
    spread_x()
    ends = []
    for side in range(2):
        low = (me.low + 1 + side) % 2
        value = back[me.x * 2 + low]
        for turn in range(2):
            wire.arrived(flow[turn, side])
            value = value + b_in[turn, side, 0].astype(F32)
        if side == 0:
            c_out[...] = value.astype(BF)
            crossed = wire.push(c_out, c_in, mate)
        else:
            ends.append(value)
    spread_x_far()
    wire.arrived(crossed)
    grad_x[...] = jnp.transpose(ends[0] + c_in[...].astype(F32))
    phase = tally["phase"]
    wire.arrived(tally["sent"])
    gain[...] = (g_out[phase] + g_in[phase]) * factor
    for turn in range(2):
        wire.arrived(ring["x"][turn])
    view = w_all.at[me.core, (me.x + 2) % 4]
    wire.push(view, view, twin)
    wire.finish()


def unpack_body(w_all, mixed, grad_x, gain, out_mixed, out_x, out_in, out_out, out_gain):
    for core in range(2):
        for part in range(4):
            value = w_all[core, part].astype(F32).reshape(256, F)
            if part < 2:
                out_out[core * F + part * 256 : core * F + part * 256 + 256] = value
            else:
                rows = slice((part - 2) * 256, (part - 2) * 256 + 256)
                out_in[rows, core * F : (core + 1) * F] = value
    out_mixed[...] = mixed[...]
    out_x[...] = grad_x[...]
    out_gain[...] = gain[...]


def shards(
    features,
    tile_vals,
    tile_row,
    tile_col,
    tile_count,
    node_type,
    type_gain,
    w_in,
    w_out,
    cotangent,
):
    row_count = lax.axis_size("row")
    col_count = lax.axis_size("col")
    hid = w_in.shape[1]
    factor = float(TILE * row_count * col_count) ** (-0.5)
    shape = jax.ShapeDtypeStruct
    vmem = pltpu.VMEM
    wide = row_count * TILE
    adjacency = build(tile_vals[0], tile_row[0], tile_col[0], tile_count[0], col_count, wide)
    space = lambda kind: pl.BlockSpec(memory_space=kind)
    copies = 128
    mixed, grad_x, w_all, gain = pl.pallas_call(
        functools.partial(layer_body, factor),
        out_shape=[
            shape((TILE, F), BF),
            shape((TILE, F), F32),
            shape((2, 4, 4, 8, 8, F), BF),
            shape((TYPES, F), F32),
        ],
        in_specs=[space(vmem), space(pl.ANY)] + [space(vmem)] * 5,
        out_specs=[space(vmem)] * 4,
        scratch_shapes=[
            vmem((row_count, TILE, F), BF),
            vmem((8, 4 * TILE, wide), BF),
            vmem((8, 2 * TILE, F), F32), vmem((8, 2 * TILE, F), F32), vmem((8, 2 * TILE, F), F32),
            vmem((2, 2, 4, TILE, F), BF), vmem((2, 2, 4, TILE, F), BF),
            vmem((TILE, F), BF), vmem((TILE, F), BF),
            vmem((F, TILE), BF), vmem((col_count, F, TILE), BF), vmem((row_count, F, TILE), F32),
            vmem((TILE, hid), F32), vmem((TILE, F), F32),
            vmem((2 * TILE, F), BF), vmem((2, TILE, F), BF), vmem((2 * TILE, F), BF),
            vmem((2, TILE, F), BF), vmem((2 * TILE, F), BF), vmem((2 * TILE, F), BF),
            vmem((4, 256, F), F32), vmem((2, 2, 256, F), BF), vmem((2, 2, 256, F), BF),
            vmem((4, 64, F), F32), vmem((2, 2, 64, F), F32), vmem((2, 2, 64, F), F32),
            vmem((8, 8, F), F32), vmem((7, 8, F), F32), vmem((8, F), BF),
            vmem((8, TYPES, F), F32), vmem((8, TYPES, F), F32),
            vmem((2, 2, 2, F, TILE), BF), vmem((2, 2, 2, F, TILE), BF),
            vmem((F, TILE), BF), vmem((F, TILE), BF),
            pltpu.SemaphoreType.DMA((32,)),
            pltpu.SemaphoreType.DMA((copies,)), pltpu.SemaphoreType.DMA((copies,)),
        ],
        compiler_params=pltpu.CompilerParams(
            collective_id=1, has_side_effects=True, vmem_limit_bytes=60 * 2**20
        ),
        name="layer",
    )(features, adjacency, cotangent, node_type[None, :], type_gain, w_in, w_out)
    mixed, grad_x, grad_w_in, grad_w_out, gain = pl.pallas_call(
        unpack_body,
        out_shape=[
            shape((TILE, F), BF), shape((TILE, F), F32), shape((F, hid), F32),
            shape((hid, F), F32), shape((TYPES, F), F32),
        ],
        name="unpack",
    )(w_all, mixed, grad_x, gain)
    return (mixed, grad_x, grad_w_in, grad_w_out, gain)


def solution(mesh):
    return jax.shard_map(
        shards,
        mesh=mesh,
        in_specs=(
            P(("col", "row"), None),
            P("row", "col", None, None),
            P("row", "col"),
            P("row", "col"),
            P("row", "col"),
            P(("row", "col")),
            P(),
            P(),
            P(),
            P(("row", "col"), None),
        ),
        out_specs=(P(("row", "col"), None), P(("col", "row"), None), P(), P(), P()),
        check_vma=False,
    )
```
